32 devices in a mesh: gx: 4 (over z), gy: 2 (over x), gz: 4 (over y, core).
Axes of the slice: x: 2, y: 2, z: 4, core: 2. Of those that a mesh axis runs over, the one named last changes fastest.
Arguments:
- queries: bfloat16 [64, 1024, 512], P(('gx', 'gy'), 'gz'), may hold values from -48 to 48
- key_vectors: bfloat16 [64, 1024, 128], P(('gx', 'gy'), 'gz'), may hold values from -12 to 12
- value_vectors: bfloat16 [64, 1024, 128], P(('gx', 'gy'), 'gz'), may hold values from -6 to 6
- chosen: int32 [64, 2], P(('gx', 'gy')), may hold values from -1 to 63, as said below
Outputs:
- attended: bfloat16 [64, 1024, 512], P(('gx', 'gy'), 'gz')
The draws below stay inside these ranges and needn't reach their ends.
Inputs may be any that keep to these rules, and one draw needn't show every extreme that they name: `chosen`: both entries of a row are -1, or both are blocks of two different groups before the row's own group, counting blocks in groups of 8 consecutive blocks. One group's rows name blocks of any one group in at most 1 entries; every group from the third on names blocks of the first group in exactly 1 entries. The rows of the first two groups are all -1.
All inputs are finite; a program needn't handle non-finite values.
Results may differ from the reference program's by a relative error of at most 0.0042.
Values may be sent and summed in bfloat16 or wider, within the bound.
No kernel may reach another device: no remote copies, remote signals or barrier semaphores. Data moves between devices by JAX's collectives and lax.ppermute only.
A program may use at most 128 MiB of HBM per device.

```python
import jax
import jax.numpy as jnp
from jax import lax

DH = 128
GROUP = 4
BLK = 1024
BG = 8
NBLK = 64


def draw_key_vectors(key, part):
    base_key = jax.random.fold_in(key, 202)
    base_draw = jnp.clip(jax.random.normal(base_key, (NBLK, BLK, DH), jnp.float32), -4.0, 4.0)
    return base_draw.astype(jnp.bfloat16)


def draw_queries(key, part):
    base_key = jax.random.fold_in(key, 303)
    base_draw = jnp.clip(jax.random.normal(base_key, (NBLK, BLK, GROUP * DH), jnp.float32), -4.0, 4.0)
    return base_draw.astype(jnp.bfloat16)


def draw_chosen(key, part):
    groups = NBLK // BG
    slot_count = 2 * BG
    perm_key, block_key = jax.random.split(jax.random.fold_in(key, 404), 2)
    shuffled = jax.vmap(lambda single: jax.random.permutation(single, groups))(jax.random.split(perm_key, groups)).astype(jnp.int32)
    group_ids = jnp.arange(groups, dtype=jnp.int32)[:, None]
    usable = (shuffled >= 1) & (shuffled < group_ids)
    order_score = jnp.where(usable, 0, groups) + jnp.arange(groups, dtype=jnp.int32)[None, :]
    ordering = jnp.argsort(order_score, axis=1)
    picked = jnp.take_along_axis(shuffled, ordering, axis=1)
    picked_ok = jnp.take_along_axis(usable, ordering, axis=1)
    padding = jnp.zeros((groups, slot_count), jnp.int32)
    picked = jnp.concatenate([picked, padding], axis=1)[:, :slot_count - 1]
    picked_ok = jnp.concatenate([picked_ok, padding > 0], axis=1)[:, :slot_count - 1]
    owner_group = jnp.concatenate([jnp.zeros((groups, 1), jnp.int32), picked], axis=1)
    owner_ok = jnp.concatenate([group_ids >= 1, picked_ok], axis=1)
    inner_pick = jax.random.randint(block_key, (groups, slot_count), 0, BG).astype(jnp.int32)
    entries = (owner_group * BG + inner_pick).reshape(groups, BG, 2)
    row_live = owner_ok.reshape(groups, BG, 2)[:, :, 1:2]
    pair = jnp.where(row_live, entries, -1)
    return pair.reshape(NBLK, 2).astype(jnp.int32)


def block_scale(own_key, dims, pieces, smallest, high):
    factor_of = 1.0
    for dim, blocks in pieces:
        draws = jax.random.uniform(jax.random.fold_in(jax.random.fold_in(own_key, 6), dim), (blocks,), jnp.float32, smallest / len(pieces), high / len(pieces))
        factor_of = factor_of * jnp.repeat(jnp.exp(draws), dims[dim] // blocks).reshape((-1,) + (1,) * (len(dims) - 1 - dim))
    return factor_of


def bell_draw(stream_key, dims, spread, reach, cuts=(), kind=jnp.bfloat16):
    values = spread * jax.random.normal(stream_key, dims, jnp.float32)
    if cuts:
        values = values * block_scale(stream_key, dims, cuts, -0.22, 0.18)
    return jnp.clip(values, -reach, reach).astype(kind)


def setup_inputs(seed: int = 0) -> dict:
    streams_of = jax.random.split(jax.random.key(seed), 5)
    queries = draw_queries(jax.random.fold_in(streams_of[4], 71), 0)
    key_vectors = draw_key_vectors(jax.random.fold_in(streams_of[4], 71), 0)
    value_vectors = bell_draw(streams_of[2], (NBLK, BLK, DH), 1.0, 6.0, ((0, 8), (1, 4)))
    chosen = draw_chosen(jax.random.fold_in(streams_of[4], 71), 0)
    return {"queries": queries, "key_vectors": key_vectors, "value_vectors": value_vectors, "chosen": chosen}


def allowed_mask(token_start, query_count, head_count, block_len, live_pair):
    token_pos = token_start + jnp.arange(query_count * head_count, dtype=jnp.int32) // head_count
    key_pos = jnp.arange(3 * block_len, dtype=jnp.int32)
    own_part = (key_pos[None, :] < block_len) & (key_pos[None, :] <= token_pos[:, None])
    pair_slot = jnp.clip(key_pos // block_len - 1, 0, 1)
    far_part = (key_pos >= block_len) & (live_pair[pair_slot] > 0)
    return own_part | far_part[None, :]


def attend_block(query_block, key_sets, value_sets, allowed):
    head_dim = key_sets.shape[1]
    flat_queries = query_block.reshape(-1, head_dim)
    scores = jnp.dot(flat_queries, key_sets.T, preferred_element_type=jnp.float32) * (head_dim ** -0.5)
    scores = jnp.where(allowed, scores, -jnp.inf)
    row_top = jnp.max(scores, axis=1, keepdims=True)
    weights = jnp.exp(scores - row_top)
    row_total = jnp.sum(weights, axis=1, keepdims=True)
    mixed = jnp.dot(weights.astype(jnp.bfloat16), value_sets, preferred_element_type=jnp.float32) / row_total
    return mixed.astype(jnp.bfloat16).reshape(query_block.shape)


def reference(queries, key_vectors, value_vectors, chosen):
    block_len = key_vectors.shape[1]
    head_dim = key_vectors.shape[2]
    head_count = queries.shape[2] // head_dim

    def one_block(block_index):
        picked_pair = chosen[block_index]
        live_pair = (picked_pair >= 0).astype(jnp.int32)
        safe_picks = jnp.maximum(picked_pair, 0)
        key_sets = jnp.concatenate([key_vectors[block_index], key_vectors[safe_picks[0]], key_vectors[safe_picks[1]]], axis=0)
        value_sets = jnp.concatenate([value_vectors[block_index], value_vectors[safe_picks[0]], value_vectors[safe_picks[1]]], axis=0)
        allowed = allowed_mask(0, block_len, head_count, block_len, live_pair)
        return attend_block(queries[block_index], key_sets, value_sets, allowed)

    return lax.map(one_block, jnp.arange(NBLK, dtype=jnp.int32))
```

```python
import functools
import math

import jax
import jax.numpy as jnp
from jax import lax
from jax.experimental import pallas as pl
from jax.experimental.pallas import tpu as pltpu
from jax.sharding import PartitionSpec as P

GROUP_AXES = ("gx", "gy")
ALL_AXES = ("gx", "gy", "gz")
F32 = jnp.float32
LOG2E = 1.4426950408889634


def plan_kernel(groups, row_slots, me_ref, chosen_ref, want_ref, meta_ref):
    blocks = chosen_ref.shape[0]
    me = me_ref[0]
    for group in range(groups):
        want_ref[group] = 0
    live = [chosen_ref[row, 0] >= 0 for row in range(blocks)]
    live_count = [jnp.int32(0)]
    for row in range(blocks):
        live_count.append(live_count[-1] + live[row].astype(jnp.int32))
    for row in range(blocks):
        place = jnp.where(live[row], live_count[row], live_count[blocks] + row - live_count[row])
        for pick in range(2):
            entry = jnp.maximum(chosen_ref[row, pick], 0)
            owner = lax.div(entry, jnp.int32(blocks))

            @pl.when(live[row])
            def _():
                want_ref[owner] = entry - owner * blocks + 1

            @pl.when(place < row_slots)
            def _():
                meta_ref[row_slots + 2 * place + pick] = jnp.where(live[row], me - owner - 1, -1)

        @pl.when(place < row_slots)
        def _():
            meta_ref[place] = jnp.int32(row)


def make_plan(chosen, me, groups, row_slots):
    smem = pl.BlockSpec(memory_space=pltpu.SMEM)
    return pl.pallas_call(
        functools.partial(plan_kernel, groups, row_slots),
        out_shape=(
            jax.ShapeDtypeStruct((groups,), jnp.int32),
            jax.ShapeDtypeStruct((3 * row_slots,), jnp.int32),
        ),
        in_specs=[smem, smem],
        out_specs=(smem, smem),
        name="plan",
    )(me, chosen)


def pick_kernel(groups, asked_ref, me_ref, key_ref, value_ref, *rest):
    outs, (buffer, in_sems, out_sems) = rest[:-3], rest[-3:]
    me = me_ref[0]
    blocks = key_ref.shape[0]

    def load(step, part):
        asked = asked_ref[lax.rem(me + step + 1, groups)]
        local = jnp.clip(asked - 1, 0, blocks - 1)
        source = (key_ref, value_ref)[part]
        return pltpu.make_async_copy(source.at[local], buffer.at[step, part], in_sems.at[step, part])

    def store(step):
        return pltpu.make_async_copy(buffer.at[step], outs[step], out_sems.at[step])

    for step in range(len(outs)):
        for part in range(2):
            load(step, part).start()
    for step in range(len(outs)):
        for part in range(2):
            load(step, part).wait()
        store(step).start()
    for step in range(len(outs)):
        store(step).wait()


def pick_blocks(asked, me, key_vectors, value_vectors, groups):
    _, quarter, head_dim = key_vectors.shape
    shifts = groups - 1
    piece = (2, quarter, head_dim)
    anywhere = pl.BlockSpec(memory_space=pl.ANY)
    smem = pl.BlockSpec(memory_space=pltpu.SMEM)
    size = 2 * shifts * math.prod(piece)
    return pl.pallas_call(
        functools.partial(pick_kernel, groups),
        out_shape=tuple(jax.ShapeDtypeStruct(piece, key_vectors.dtype) for _ in range(shifts)),
        in_specs=[smem, smem, anywhere, anywhere],
        out_specs=tuple(anywhere for _ in range(shifts)),
        scratch_shapes=[
            pltpu.VMEM((shifts,) + piece, key_vectors.dtype),
            pltpu.SemaphoreType.DMA((shifts, 2)),
            pltpu.SemaphoreType.DMA((shifts,)),
        ],
        cost_estimate=pl.CostEstimate(flops=0, bytes_accessed=2 * size, transcendentals=0),
        name="pick",
    )(asked, me, key_vectors, value_vectors)


def soften(query, pieces, state, scale, masked):
    scores = []
    for index, (keys, _) in enumerate(pieces):
        score = lax.dot_general(
            query, keys, (((1,), (1,)), ((), ())), preferred_element_type=F32
        )
        if masked and index == 0:
            token = lax.broadcasted_iota(jnp.int32, score.shape, 0)
            key = lax.broadcasted_iota(jnp.int32, score.shape, 1)
            score = jnp.where(key <= token, score, -jnp.inf)
        scores.append(score)
    top = functools.reduce(jnp.maximum, scores)
    top = jnp.max(top, axis=1, keepdims=True)
    if state is not None:
        top = jnp.maximum(top, state[0])
    total = None
    mixed = None
    for score, (_, values) in zip(scores, pieces):
        weight = jnp.exp2((score - top) * scale)
        part = jnp.sum(weight, axis=1, keepdims=True)
        product = jnp.dot(weight.astype(values.dtype), values, preferred_element_type=F32)
        total = part if total is None else total + part
        mixed = product if mixed is None else mixed + product
    if state is not None:
        fade = jnp.exp2((state[0] - top) * scale)
        total = total + state[1] * fade
        mixed = mixed + state[2] * fade
    return top, total, mixed


class Store:
    def __init__(self, stat_ref, mix_ref, heads, head_dim):
        self.stat_ref, self.mix_ref = stat_ref, mix_ref
        self.heads, self.head_dim = heads, head_dim

    def get(self, head):
        low = head * self.head_dim
        return (
            self.stat_ref[0, :, head : head + 1],
            self.stat_ref[0, :, self.heads + head : self.heads + head + 1],
            self.mix_ref[0, :, low : low + self.head_dim],
        )

    def put(self, head, state):
        low = head * self.head_dim
        self.stat_ref[0, :, head : head + 1] = state[0]
        self.stat_ref[0, :, self.heads + head : self.heads + head + 1] = state[1]
        self.mix_ref[0, :, low : low + self.head_dim] = state[2]


def update(store, query_ref, pieces, scale, fresh, masked):
    for head in range(store.heads):
        low = head * store.head_dim
        query = query_ref[0, :, low : low + store.head_dim]
        state = None if fresh else store.get(head)
        store.put(head, soften(query, pieces, state, scale, masked))


def finish(store, out_ref):
    for head in range(store.heads):
        _, total, mixed = store.get(head)
        low = head * store.head_dim
        out_ref[0, :, low : low + store.head_dim] = (mixed / total).astype(out_ref.dtype)


def own_kernel(heads, bits, fresh, place_ref, *refs):
    refs = list(refs)
    query_ref = refs.pop(0)
    head_dim = query_ref.shape[2] // heads
    scale = LOG2E * head_dim**-0.5
    quarter_index = place_ref[0]

    def take(count):
        taken = [refs.pop(0) for _ in range(2 * count)]
        return lambda: [(taken[2 * i][0], taken[2 * i + 1][0]) for i in range(count)]

    first = take(1) if fresh else None
    higher = [(bit, take(bit)) for bit in bits]
    if not fresh:
        old = [refs.pop(0), refs.pop(0)]
    if len(refs) == 3:
        out_ref, stat_ref, mix_ref = refs
    else:
        out_ref, (stat_ref, mix_ref) = None, refs
    store = Store(stat_ref, mix_ref, heads, head_dim)
    if fresh:
        update(store, query_ref, first(), scale, True, True)
    else:
        stat_ref[...] = old[0][...]
        mix_ref[...] = old[1][...]
    for bit, pieces in higher:

        @pl.when((quarter_index & bit) != 0)
        def _():
            update(store, query_ref, pieces(), scale, False, False)

    if out_ref is not None:
        finish(store, out_ref)


def own_call(queries, quarter_index, heads, pieces_of, bits, state, emit, name):
    blocks, quarter, width = queries.shape
    head_dim = width // heads
    fresh = state is None
    masks = ([0] if fresh else []) + [m for bit in bits for m in range(bit, 2 * bit)]
    operands = [queries]
    row = lambda i, *_: (i, 0, 0)
    specs = [pl.BlockSpec((1, quarter, width), row)]
    for mask in masks:
        operands += list(pieces_of[mask])
        specs += [pl.BlockSpec((1, quarter, head_dim), row)] * 2
    if not fresh:
        operands += list(state)
        specs += [pl.BlockSpec((1, quarter, 128), row), pl.BlockSpec((1, quarter, width), row)]
    out_shape = [
        jax.ShapeDtypeStruct((blocks, quarter, 128), F32),
        jax.ShapeDtypeStruct((blocks, quarter, width), F32),
    ]
    out_specs = [pl.BlockSpec((1, quarter, 128), row), pl.BlockSpec((1, quarter, width), row)]
    if emit:
        out_shape.insert(0, jax.ShapeDtypeStruct(queries.shape, queries.dtype))
        out_specs.insert(0, pl.BlockSpec((1, quarter, width), row))
    work = blocks * heads * quarter * quarter * len(masks)
    return pl.pallas_call(
        functools.partial(own_kernel, heads, bits, fresh),
        out_shape=tuple(out_shape),
        grid_spec=pltpu.PrefetchScalarGridSpec(
            num_scalar_prefetch=1,
            grid=(blocks,),
            in_specs=specs,
            out_specs=tuple(out_specs),
        ),
        compiler_params=pltpu.CompilerParams(dimension_semantics=("arbitrary",)),
        cost_estimate=pl.CostEstimate(
            flops=4 * work * head_dim, bytes_accessed=8 * queries.size, transcendentals=work
        ),
        name=name,
    )(quarter_index, *operands)


def far_kernel(heads, row_slots, low, high, kinds, emit, meta_ref, *refs):
    refs = list(refs)
    query_ref = refs.pop(0)
    head_dim = query_ref.shape[2] // heads
    scale = LOG2E * head_dim**-0.5
    step = pl.program_id(0)
    picks = [[refs.pop(0) for _ in range(kinds)] for _ in range(2)]
    old = [refs.pop(0), refs.pop(0)]
    if emit:
        refs.pop(0)
        out_ref, stat_ref, mix_ref = refs
    else:
        out_ref, (stat_ref, mix_ref) = None, refs
    store = Store(stat_ref, mix_ref, heads, head_dim)
    stat_ref[...] = old[0][...]
    mix_ref[...] = old[1][...]
    for pick in range(2):
        slot = meta_ref[row_slots + 2 * step + pick]

        @pl.when((slot >= low) & (slot < high))
        def _():
            pieces = [(ref[0], ref[1]) for ref in picks[pick]]
            update(store, query_ref, pieces, scale, False, False)

    if emit:
        finish(store, out_ref)


def far_call(queries, meta, heads, row_slots, low, high, stacks, state, out, name):
    blocks, quarter, width = queries.shape
    head_dim = width // heads
    emit = out is not None
    row = lambda i, meta: (meta[i], 0, 0)
    query_spec = pl.BlockSpec((1, quarter, width), row)
    stat_spec = pl.BlockSpec((1, quarter, 128), row)
    specs = [query_spec]
    operands = [queries]
    for pick in range(2):

        def slot(i, meta, pick=pick):
            return (jnp.clip(meta[row_slots + 2 * i + pick] - low, 0, high - low - 1), 0, 0)

        specs += [pl.BlockSpec((2, quarter, head_dim), slot)] * len(stacks)
        operands += stacks
    aliases = {len(operands) + 1: 0, len(operands) + 2: 1}
    operands += list(state)
    specs += [stat_spec, query_spec]
    out_shape = [jax.ShapeDtypeStruct(part.shape, part.dtype) for part in state]
    out_specs = [stat_spec, query_spec]
    if emit:
        aliases = {key: value + 1 for key, value in aliases.items()}
        aliases[len(operands) + 1] = 0
        operands.append(out)
        specs.append(pl.BlockSpec(memory_space=pl.ANY))
        out_shape.insert(0, jax.ShapeDtypeStruct(out.shape, out.dtype))
        out_specs.insert(0, query_spec)
    work = row_slots * heads * quarter * quarter * len(stacks)
    return pl.pallas_call(
        functools.partial(far_kernel, heads, row_slots, low, high, len(stacks), emit),
        out_shape=tuple(out_shape),
        grid_spec=pltpu.PrefetchScalarGridSpec(
            num_scalar_prefetch=1, grid=(row_slots,), in_specs=specs, out_specs=tuple(out_specs)
        ),
        input_output_aliases=aliases,
        compiler_params=pltpu.CompilerParams(dimension_semantics=("arbitrary",)),
        cost_estimate=pl.CostEstimate(
            flops=4 * work * head_dim, bytes_accessed=4 * queries.size, transcendentals=work
        ),
        name=name,
    )(meta, *operands)


def body(quarters, groups, queries, key_vectors, value_vectors, chosen):
    blocks, quarter, width = queries.shape
    head_dim = key_vectors.shape[2]
    heads = width // head_dim
    row_slots = min(blocks, (groups - 1) // 2)
    shifts = groups - 1
    me = lax.axis_index(GROUP_AXES).reshape(1).astype(jnp.int32)
    quarter_index = lax.axis_index("gz").reshape(1).astype(jnp.int32)
    bits = [1 << i for i in range(quarters.bit_length() - 1)]

    def own_send(part, mask, bit):
        pairs = [
            (group * quarters + (q ^ bit), group * quarters + q)
            for group in range(groups)
            for q in range(quarters)
            if q ^ mask < q
        ]
        return lax.ppermute(part, ALL_AXES, pairs)

    def far_send(part, bit):
        pairs = [
            (group * quarters + (q ^ bit), group * quarters + q)
            for group in range(2, groups)
            for q in range(quarters)
        ]
        return lax.ppermute(part, ALL_AXES, pairs)

    def shift_send(part, shift):
        pairs = [
            (group * quarters + q, (group + shift) * quarters + q)
            for group in range(groups)
            for q in range(quarters)
            if 2 <= group + shift < groups
        ]
        return lax.ppermute(part, ALL_AXES, pairs)

    own = {0: (key_vectors, value_vectors)}
    top = bits[-1]
    own[top] = tuple(own_send(part, top, top) for part in own[0])

    want, meta = make_plan(chosen, me, groups, row_slots)
    asked = lax.all_to_all(want, GROUP_AXES, split_axis=0, concat_axis=0, tiled=True)
    picked = pick_blocks(asked, me, key_vectors, value_vectors, groups)
    arrived = [shift_send(part, index + 1) for index, part in enumerate(picked)]

    for bit in bits[:-1][::-1]:
        for mask in [0] + [m for m in own if m]:
            if mask & bit == 0:
                own[mask | bit] = tuple(own_send(part, mask | bit, bit) for part in own[mask])
    state = own_call(queries, quarter_index, heads, own, bits[:-1], None, False, "own_near")
    out, *state = own_call(queries, quarter_index, heads, own, bits[-1:], state, True, "own_far")

    half = (shifts + 1) // 2
    batches = [(0, half), (half, shifts)]
    for index, (low, high) in enumerate(batches):
        stacks = [jnp.concatenate(arrived[low:high], axis=0)]
        for bit in bits[::-1]:
            stacks += [far_send(stack, bit) for stack in stacks]
        last = index == len(batches) - 1
        result = far_call(
            queries, meta, heads, row_slots, low, high, stacks, state, out if last else None, f"far_{index}"
        )
        if last:
            out = result[0]
        else:
            state = result
    return out


def solution(mesh):
    placed = (
        P(GROUP_AXES, "gz", None),
        P(GROUP_AXES, "gz", None),
        P(GROUP_AXES, "gz", None),
        P(GROUP_AXES, None),
    )
    groups = mesh.shape["gx"] * mesh.shape["gy"]
    return jax.shard_map(
        functools.partial(body, mesh.shape["gz"], groups),
        mesh=mesh,
        in_specs=placed,
        out_specs=P(GROUP_AXES, "gz", None),
        check_vma=False,
    )
```
